32 devices in a mesh: dp: 32 (over z, y, x, core).
Axes of the slice: x: 2, y: 2, z: 4, core: 2. Of those that a mesh axis runs over, the one named last changes fastest.
Arguments:
- tokens: bfloat16 [8192, 960], P('dp'), may hold values from -6 to 6
- out_grad: bfloat16 [8192, 960], P('dp'), may hold values from -6 to 6
- segment_ids: int32 [32, 256], P('dp'), may hold values from 0 to 255, as said below
- positions: int32 [32, 256], P('dp'), may hold values from 0 to 255, as said below
- attn_weight: bfloat16 [960, 2560], P(None, 'dp'), as said below
- gate_weight: bfloat16 [960, 2560], P(None, 'dp'), may hold values from -0.1875 to 0.1875
- up_weight: bfloat16 [960, 2560], P(None, 'dp'), may hold values from -0.1875 to 0.1875
- down_weight: bfloat16 [2560, 960], P('dp'), may hold values from -0.15625 to 0.15625
- norm_gains: bfloat16 [1920], P('dp'), may hold values from 0.25 to 1.75
Outputs:
- block_out: bfloat16 [8192, 960], P('dp')
- tokens_grad: float32 [8192, 960], P('dp')
- attn_weight_grad: float32 [960, 2560], P(None, 'dp')
- gate_weight_grad: float32 [960, 2560], P(None, 'dp')
- up_weight_grad: float32 [960, 2560], P(None, 'dp')
- down_weight_grad: float32 [2560, 960], P('dp')
- norm_gains_grad: float32 [1920], P('dp')
The draws below stay inside these ranges and needn't reach their ends.
Inputs may be any that keep to these rules, and one draw needn't show every extreme that they name: `segment_ids`: in every sequence the ids start at 0 and rise by one where a new document begins; some sequence has a new document at every token. `positions`: A token's offset from the first token of its document; some sequence is a single document. `attn_weight`: projection weights scaled by their fan-in.
All inputs are finite; a program needn't handle non-finite values.
Results may differ from the reference program's by a relative error of at most 0.01.
The reference program's roundings to bfloat16 on the way count: a program that leaves them out, or rounds other values in their place, can miss the bound.
Values may be sent and summed in bfloat16 or wider, within the bound.
A program may use at most 256 MiB of HBM per device.

```python
import jax
import jax.numpy as jnp
from jax import lax

D = 960
HEADS = 15
KV_HEADS = 5
HEAD_DIM = 64
FF = 2560
SEQ = 256
GROUP = 3
QD = 960
KD = 320
ATTN_COLS = 2560
SEQS = 32
TOKENS = 8192


def segment_layout(key):
    token_index = jnp.arange(SEQ, dtype=jnp.int32)
    seq_index = jnp.arange(SEQS, dtype=jnp.int32)[:, None]
    starts = jax.random.randint(jax.random.fold_in(key, 11), (SEQS, SEQ), 0, max(SEQ // 4, 2)) == 0
    starts = starts | (token_index[None, :] == 0)
    starts = jnp.where(seq_index == 0, token_index[None, :] == 0, starts)
    starts = jnp.where(seq_index == 1, True, starts)
    segments = jnp.cumsum(starts.astype(jnp.int32), axis=1) - 1
    doc_begin = lax.cummax(jnp.where(starts, token_index[None, :], 0), axis=1)
    return (segments.astype(jnp.int32), (token_index[None, :] - doc_begin).astype(jnp.int32))


def draw_segment_ids(key, part):
    return segment_layout(key)[0]


def draw_positions(key, part):
    return segment_layout(key)[1]


def draw_attn_weight(key, part):
    entries = jnp.clip(jax.random.normal(key, (D, ATTN_COLS), jnp.float32), -6.0, 6.0)
    column = jnp.arange(ATTN_COLS)
    col_scale = jnp.where(column < QD + KD, D ** (-0.5), jnp.where(column < QD + 2 * KD, D ** (-0.5), 6.0 * QD ** (-0.5)))
    return (entries * col_scale[None, :]).astype(jnp.bfloat16)


def spiked(values, key, source, target, parts, factor):
    owner, partner = [(jnp.arange(values.shape[dim]) // (values.shape[dim] // parts)).reshape([-1 if axis == dim else 1 for axis in range(values.ndim)]) for dim in (source, target)]
    chosen = jax.random.permutation(key, parts)[partner]
    strong = (owner == chosen) | (owner == (partner + parts // 2) % parts)
    return jnp.where(strong, factor * values, values)


def shard_levels(key, extent, pieces, smallest, high):
    def one(position, parts):
        steps = jax.random.uniform(jax.random.fold_in(jax.random.fold_in(key, 6), position), (parts,), jnp.float32, smallest / len(pieces), high / len(pieces))
        return jnp.repeat(jnp.exp(steps), extent[position] // parts).reshape((-1,) + (1,) * (len(extent) - position - 1))

    level = one(*pieces[0])
    for cut in pieces[1:]:
        level = level * one(*cut)
    return level


def noise(key, extent, spread, reach, shards=(), held_as=jnp.bfloat16):
    factor_of = shard_levels(key, extent, shards, -0.22, 0.18) if shards else 1.0
    values = jax.random.normal(key, extent, jnp.float32) * spread * factor_of
    return jnp.minimum(jnp.maximum(values, -reach), reach).astype(held_as)


def bell_draw_with(own_key, shape, spread, most, split, heavy, kind=jnp.bfloat16):
    values = spread * jax.random.normal(own_key, shape, jnp.float32)
    if split:
        values = values * shard_levels(own_key, shape, split, -0.22, 0.18)
    return jnp.clip(spiked(values, jax.random.fold_in(own_key, 3), *heavy), -most, most).astype(kind)


def setup_inputs(seed: int = 0) -> dict:
    streams_of = jax.random.split(jax.random.key(seed), 10)
    tokens = noise(streams_of[0], (TOKENS, D), 1.0, 6.0, ((0, 32),))
    out_grad = bell_draw_with(streams_of[1], (TOKENS, D), 1.0, 6.0, ((0, 32),), (0, 1, 32, 2.75))
    segment_ids = draw_segment_ids(jax.random.fold_in(streams_of[9], 71), 0)
    positions = draw_positions(jax.random.fold_in(streams_of[9], 71), 0)
    attn_weight = draw_attn_weight(jax.random.fold_in(streams_of[9], 71), 0)
    gate_weight = noise(streams_of[5], (D, FF), D ** -0.5, 0.1875, ((1, 32),))
    up_weight = noise(streams_of[6], (D, FF), D ** -0.5, 0.1875, ((1, 32),))
    down_weight = noise(streams_of[7], (FF, D), (FF // 2) ** -0.5, 0.15625, ((0, 32),))
    norm_gains = jnp.clip(1.0 + 0.15 * jax.random.normal(streams_of[8], (2 * D,), jnp.float32), 0.25, 1.75).astype(jnp.bfloat16)
    return dict(tokens=tokens, out_grad=out_grad, segment_ids=segment_ids, positions=positions, attn_weight=attn_weight, gate_weight=gate_weight, up_weight=up_weight, down_weight=down_weight, norm_gains=norm_gains)


epsilon = 1e-05
rope_base = 10000.0
masked_score = -1e+30

def product(form, left, right):
    return jnp.einsum(form, left.astype(jnp.float32), right.astype(jnp.float32))

def contract(left, right, left_axis, right_axis):
    return lax.dot_general(left, right, (((left_axis,), (right_axis,)), ((), ())), preferred_element_type=jnp.float32)

def rotate_half(values):
    half_dim = values.shape[-1] // 2
    return jnp.concatenate([-values[..., half_dim:], values[..., :half_dim]], axis=-1)

def rope_tables(positions):
    half_dim = HEAD_DIM // 2
    inverse = rope_base ** (-2.0 * jnp.arange(half_dim).astype(jnp.float32) / HEAD_DIM)
    angles = positions.astype(jnp.float32)[:, None] * inverse[None, :]
    angles = jnp.concatenate([angles, angles], axis=-1)
    return (jnp.cos(angles)[:, None, :], jnp.sin(angles)[:, None, :])

def norm_rows(values, gain):
    inv_rms = lax.rsqrt(lax.optimization_barrier(jnp.mean(values * values, axis=-1, keepdims=True)) + epsilon)
    normed = values * inv_rms
    return (normed, inv_rms, (normed * gain.astype(jnp.float32)).astype(jnp.bfloat16))

def norm_back(grad_in, normed, inv_rms, gain):
    grad_normed = grad_in * gain.astype(jnp.float32)
    grad_gain = lax.optimization_barrier(jnp.sum(grad_in * normed, axis=0))
    inner_mean = lax.optimization_barrier(jnp.mean(grad_normed * normed, axis=-1, keepdims=True))
    return (inv_rms * (grad_normed - normed * inner_mean), grad_gain)

def allowed_pairs(segments):
    row_index = jnp.arange(segments.shape[0])
    same_doc = segments[:, None] == segments[None, :]
    return same_doc & (row_index[:, None] >= row_index[None, :])

def scores_of(queries, key_rows, allowed):
    scores = product('qhgd,shd->hgqs', queries, key_rows) * HEAD_DIM ** (-0.5)
    return jnp.where(allowed[None, None], scores, masked_score)

def attend(queries, key_rows, value_rows, allowed):
    scores = scores_of(queries, key_rows, allowed)
    row_max = lax.optimization_barrier(jnp.max(scores, axis=-1, keepdims=True))
    weights = jnp.exp(scores - row_max)
    totals = lax.optimization_barrier(jnp.sum(weights, axis=-1, keepdims=True))
    weights_low = (weights / totals).astype(jnp.bfloat16)
    mixed_heads = product('hgqs,shd->qhgd', weights_low, value_rows).astype(jnp.bfloat16)
    return (mixed_heads, row_max + jnp.log(totals))

def attend_back(queries, key_rows, value_rows, allowed, mixed_heads, log_totals, grad_heads):
    scores = scores_of(queries, key_rows, allowed)
    probs_back = jnp.exp(scores - log_totals)
    grad_values = product('hgqs,qhgd->shd', probs_back.astype(jnp.bfloat16), grad_heads)
    grad_probs = product('qhgd,shd->hgqs', grad_heads, value_rows)
    row_dot = lax.optimization_barrier(jnp.sum(grad_heads.astype(jnp.float32) * mixed_heads.astype(jnp.float32), axis=-1))
    row_dot = jnp.transpose(row_dot, (1, 2, 0))[..., None]
    grad_scores = (probs_back * (grad_probs - row_dot) * HEAD_DIM ** (-0.5)).astype(jnp.bfloat16)
    grad_queries = product('hgqs,shd->qhgd', grad_scores, key_rows)
    grad_keys = product('hgqs,qhgd->shd', grad_scores, queries)
    return (grad_queries, grad_keys, grad_values)

def layer_forward(tokens, segments, positions, attn_weight, gate_weight, up_weight, down_weight, norm_gains):
    seq_len = tokens.shape[0]
    model_width = tokens.shape[1]
    residual = tokens.astype(jnp.float32)
    normed_one, inv_one, input_one = norm_rows(residual, norm_gains[:model_width])
    projected = contract(input_one, attn_weight[:, :QD + 2 * KD], 1, 0)
    cosine, sine_tab = rope_tables(positions)
    query_part = projected[:, :QD].reshape(seq_len, HEADS, HEAD_DIM)
    key_part = projected[:, QD:QD + KD].reshape(seq_len, KV_HEADS, HEAD_DIM)
    queries = (query_part * cosine + rotate_half(query_part) * sine_tab).astype(jnp.bfloat16)
    queries = queries.reshape(seq_len, KV_HEADS, GROUP, HEAD_DIM)
    key_rows = (key_part * cosine + rotate_half(key_part) * sine_tab).astype(jnp.bfloat16)
    value_rows = projected[:, QD + KD:].reshape(seq_len, KV_HEADS, HEAD_DIM).astype(jnp.bfloat16)
    allowed = allowed_pairs(segments)
    mixed_heads, log_totals = attend(queries, key_rows, value_rows, allowed)
    mixed_flat = mixed_heads.reshape(seq_len, QD)
    middle = residual + contract(mixed_flat, attn_weight[:, QD + 2 * KD:], 1, 1)
    normed_two, inv_two, input_two = norm_rows(middle, norm_gains[model_width:])
    gate_act = contract(input_two, gate_weight, 1, 0)
    up_proj = contract(input_two, up_weight, 1, 0)
    hidden = (jax.nn.silu(gate_act) * up_proj).astype(jnp.bfloat16)
    output = middle + contract(hidden, down_weight, 1, 0)
    kept_state = {'normed_one': normed_one, 'inv_one': inv_one, 'input_one': input_one, 'cosine': cosine, 'sine_tab': sine_tab, 'queries': queries, 'key_rows': key_rows, 'value_rows': value_rows, 'allowed': allowed, 'mixed_heads': mixed_heads, 'log_totals': log_totals, 'normed_two': normed_two, 'inv_two': inv_two, 'input_two': input_two, 'gate_act': gate_act, 'up_proj': up_proj, 'hidden': hidden}
    return (output.astype(jnp.bfloat16), kept_state)

def ffn_backward(out_grad, kept_state, gate_weight, up_weight, down_weight, norm_gains):
    model_width = out_grad.shape[1]
    gate_act = kept_state['gate_act']
    input_two = kept_state['input_two']
    grad_hidden = contract(out_grad, down_weight, 1, 1)
    grad_down = contract(kept_state['hidden'], out_grad, 0, 0)
    sig_gate = jax.nn.sigmoid(gate_act)
    grad_gate = (grad_hidden * kept_state['up_proj'] * sig_gate * (1.0 + gate_act * (1.0 - sig_gate))).astype(jnp.bfloat16)
    grad_up = (grad_hidden * gate_act * sig_gate).astype(jnp.bfloat16)
    grad_gate_w = contract(input_two, grad_gate, 0, 0)
    grad_up_w = contract(input_two, grad_up, 0, 0)
    grad_input_two = contract(grad_gate, gate_weight, 1, 1) + contract(grad_up, up_weight, 1, 1)
    grad_norm_two, grad_gain_two = norm_back(grad_input_two, kept_state['normed_two'], kept_state['inv_two'], norm_gains[model_width:])
    grad_middle = out_grad.astype(jnp.float32) + grad_norm_two
    return (grad_middle, grad_gain_two, (grad_gate_w, grad_up_w, grad_down))

def attn_backward(grad_middle, kept_state, attn_weight, norm_gains):
    seq_len = grad_middle.shape[0]
    model_width = grad_middle.shape[1]
    mixed_heads = kept_state['mixed_heads']
    grad_mid_low = grad_middle.astype(jnp.bfloat16)
    grad_out_proj = contract(grad_mid_low, mixed_heads.reshape(seq_len, QD), 0, 0)
    grad_heads = contract(grad_mid_low, attn_weight[:, QD + 2 * KD:], 1, 0).astype(jnp.bfloat16)
    grad_heads = grad_heads.reshape(seq_len, KV_HEADS, GROUP, HEAD_DIM)
    grad_queries, grad_keys, grad_values = attend_back(kept_state['queries'], kept_state['key_rows'], kept_state['value_rows'], kept_state['allowed'], mixed_heads, kept_state['log_totals'], grad_heads)
    cosine = kept_state['cosine']
    sine_tab = kept_state['sine_tab']
    grad_q_part = grad_queries.reshape(seq_len, HEADS, HEAD_DIM)
    grad_q_part = grad_q_part * cosine - rotate_half(grad_q_part) * sine_tab
    grad_k_part = grad_keys * cosine - rotate_half(grad_keys) * sine_tab
    grad_projected = jnp.concatenate([grad_q_part.reshape(seq_len, QD), grad_k_part.reshape(seq_len, KD), grad_values.reshape(seq_len, KD)], axis=1).astype(jnp.bfloat16)
    grad_qkv = contract(kept_state['input_one'], grad_projected, 0, 0)
    grad_input_one = contract(grad_projected, attn_weight[:, :QD + 2 * KD], 1, 1)
    grad_norm_one, grad_gain_one = norm_back(grad_input_one, kept_state['normed_one'], kept_state['inv_one'], norm_gains[:model_width])
    grad_tokens = grad_middle + grad_norm_one
    grad_attn = jnp.concatenate([grad_qkv, grad_out_proj], axis=1)
    return (grad_tokens, grad_attn, grad_gain_one)

def reference(tokens, out_grad, segment_ids, positions, attn_weight, gate_weight, up_weight, down_weight, norm_gains):
    token_seqs = tokens.reshape(SEQS, SEQ, D)
    grad_seqs = out_grad.reshape(SEQS, SEQ, D)

    def one_sequence(totals, inputs):
        seq_tokens, seq_grad, seq_segments, seq_positions = inputs
        output, kept_state = layer_forward(seq_tokens, seq_segments, seq_positions, attn_weight, gate_weight, up_weight, down_weight, norm_gains)
        grad_middle, grad_gain_two, ffn_grads = ffn_backward(seq_grad, kept_state, gate_weight, up_weight, down_weight, norm_gains)
        grad_tokens, grad_attn, grad_gain_one = attn_backward(grad_middle, kept_state, attn_weight, norm_gains)
        seq_terms = (grad_attn, ffn_grads[0], ffn_grads[1], ffn_grads[2], jnp.concatenate([grad_gain_one, grad_gain_two]))
        return (jax.tree.map(jnp.add, totals, seq_terms), (output, grad_tokens))
    zero_grads = (jnp.zeros((D, ATTN_COLS), jnp.float32), jnp.zeros((D, FF), jnp.float32), jnp.zeros((D, FF), jnp.float32), jnp.zeros((FF, D), jnp.float32), jnp.zeros((2 * D,), jnp.float32))
    totals, stacked = lax.scan(one_sequence, zero_grads, (token_seqs, grad_seqs, segment_ids, positions))
    outputs = stacked[0].reshape(TOKENS, D)
    grad_tokens = stacked[1].reshape(TOKENS, D)
    return (outputs, grad_tokens, totals[0], totals[1], totals[2], totals[3], totals[4])
```

```python
import jax
import jax.numpy as jnp
from jax import lax
from jax.experimental import pallas as pl
from jax.experimental.pallas import tpu as pltpu
from jax.sharding import PartitionSpec as P

HEADS = 15
KV_HEADS = 5
HEAD_DIM = 64
GROUP = 3
QD = 960
KD = 320


epsilon = 1e-05
rope_base = 10000.0
masked_score = -1e30


def product(form, left, right):
    return jnp.einsum(form, left, right, preferred_element_type=jnp.float32)


def contract(left, right, left_axis, right_axis):
    return lax.dot_general(
        left, right, (((left_axis,), (right_axis,)), ((), ())), preferred_element_type=jnp.float32
    )


def rotate_half(values):
    half_dim = values.shape[-1] // 2
    return jnp.concatenate([-values[..., half_dim:], values[..., :half_dim]], axis=-1)


def rope_tables(positions):
    half_dim = HEAD_DIM // 2
    inverse = rope_base ** (-2.0 * jnp.arange(half_dim).astype(jnp.float32) / HEAD_DIM)
    angles = positions.astype(jnp.float32)[:, None] * inverse[None, :]
    angles = jnp.concatenate([angles, angles], axis=-1)
    return (jnp.cos(angles)[:, None, :], jnp.sin(angles)[:, None, :])


def norm_rows(values, gain):
    inv_rms = lax.rsqrt(jnp.mean(values * values, axis=-1, keepdims=True) + epsilon)
    normed = values * inv_rms
    return (normed, inv_rms, (normed * gain.astype(jnp.float32)).astype(jnp.bfloat16))


def norm_back(grad_in, normed, inv_rms, gain):
    grad_normed = grad_in * gain.astype(jnp.float32)
    grad_gain = jnp.sum(grad_in * normed, axis=0)
    inner_mean = jnp.mean(grad_normed * normed, axis=-1, keepdims=True)
    return (inv_rms * (grad_normed - normed * inner_mean), grad_gain)


def allowed_pairs(segments):
    row_index = jnp.arange(segments.shape[0])
    same_doc = segments[:, None] == segments[None, :]
    return same_doc & (row_index[:, None] >= row_index[None, :])


def scores_of(queries, key_rows, allowed):
    scores = product("qhgd,shd->hgqs", queries, key_rows) * HEAD_DIM ** (-0.5)
    return jnp.where(allowed[None, None], scores, masked_score)


def attend(queries, key_rows, value_rows, allowed):
    scores = scores_of(queries, key_rows, allowed)
    row_max = jnp.max(scores, axis=-1, keepdims=True)
    weights = jnp.exp(scores - row_max)
    totals = jnp.sum(weights, axis=-1, keepdims=True)
    weights_low = (weights / totals).astype(jnp.bfloat16)
    mixed_heads = product("hgqs,shd->qhgd", weights_low, value_rows).astype(jnp.bfloat16)
    return (mixed_heads, row_max + jnp.log(totals))


def attend_back(queries, key_rows, value_rows, allowed, mixed_heads, log_totals, grad_heads):
    scores = scores_of(queries, key_rows, allowed)
    probs_back = jnp.exp(scores - log_totals)
    grad_values = product("hgqs,qhgd->shd", probs_back.astype(jnp.bfloat16), grad_heads)
    grad_probs = product("qhgd,shd->hgqs", grad_heads, value_rows)
    row_dot = jnp.sum(grad_heads.astype(jnp.float32) * mixed_heads.astype(jnp.float32), axis=-1)
    row_dot = jnp.transpose(row_dot, (1, 2, 0))[..., None]
    grad_scores = (probs_back * (grad_probs - row_dot) * HEAD_DIM ** (-0.5)).astype(jnp.bfloat16)
    grad_queries = product("hgqs,shd->qhgd", grad_scores, key_rows)
    grad_keys = product("hgqs,qhgd->shd", grad_scores, queries)
    return (grad_queries, grad_keys, grad_values)


def layer_forward(
    tokens, segments, positions, attn_rows, gate_rows, up_rows, down_weight, norm_gains
):
    seq_len = tokens.shape[0]
    model_width = tokens.shape[1]
    residual = tokens.astype(jnp.float32)
    normed_one, inv_one, input_one = norm_rows(residual, norm_gains[:model_width])
    projected = contract(input_one, attn_rows[: QD + 2 * KD], 1, 1)
    cosine, sine_tab = rope_tables(positions)
    query_part = projected[:, :QD].reshape(seq_len, HEADS, HEAD_DIM)
    key_part = projected[:, QD : QD + KD].reshape(seq_len, KV_HEADS, HEAD_DIM)
    queries = (query_part * cosine + rotate_half(query_part) * sine_tab).astype(jnp.bfloat16)
    queries = queries.reshape(seq_len, KV_HEADS, GROUP, HEAD_DIM)
    key_rows = (key_part * cosine + rotate_half(key_part) * sine_tab).astype(jnp.bfloat16)
    value_rows = projected[:, QD + KD :].reshape(seq_len, KV_HEADS, HEAD_DIM).astype(jnp.bfloat16)
    allowed = allowed_pairs(segments)
    mixed_heads, log_totals = attend(queries, key_rows, value_rows, allowed)
    mixed_flat = mixed_heads.reshape(seq_len, QD)
    middle = residual + contract(mixed_flat, attn_rows[QD + 2 * KD :], 1, 0)
    normed_two, inv_two, input_two = norm_rows(middle, norm_gains[model_width:])
    gate_act = contract(input_two, gate_rows, 1, 1)
    up_proj = contract(input_two, up_rows, 1, 1)
    hidden = (jax.nn.silu(gate_act) * up_proj).astype(jnp.bfloat16)
    output = middle + contract(hidden, down_weight, 1, 0)
    kept_state = {
        "normed_one": normed_one,
        "inv_one": inv_one,
        "input_one": input_one,
        "cosine": cosine,
        "sine_tab": sine_tab,
        "queries": queries,
        "key_rows": key_rows,
        "value_rows": value_rows,
        "allowed": allowed,
        "mixed_heads": mixed_heads,
        "log_totals": log_totals,
        "normed_two": normed_two,
        "inv_two": inv_two,
        "input_two": input_two,
        "gate_act": gate_act,
        "up_proj": up_proj,
        "hidden": hidden,
    }
    return (output.astype(jnp.bfloat16), kept_state)


def ffn_backward(out_grad, kept_state, gate_rows, up_rows, down_weight, norm_gains):
    model_width = out_grad.shape[1]
    gate_act = kept_state["gate_act"]
    input_two = kept_state["input_two"]
    grad_hidden = contract(out_grad, down_weight, 1, 1)
    grad_down = contract(kept_state["hidden"], out_grad, 0, 0)
    sig_gate = jax.nn.sigmoid(gate_act)
    grad_gate = (
        grad_hidden * kept_state["up_proj"] * sig_gate * (1.0 + gate_act * (1.0 - sig_gate))
    ).astype(jnp.bfloat16)
    grad_up = (grad_hidden * gate_act * sig_gate).astype(jnp.bfloat16)
    grad_gate_w = contract(grad_gate, input_two, 0, 0)
    grad_up_w = contract(grad_up, input_two, 0, 0)
    grad_input_two = contract(grad_gate, gate_rows, 1, 0) + contract(grad_up, up_rows, 1, 0)
    grad_norm_two, grad_gain_two = norm_back(
        grad_input_two, kept_state["normed_two"], kept_state["inv_two"], norm_gains[model_width:]
    )
    grad_middle = out_grad.astype(jnp.float32) + grad_norm_two
    return (grad_middle, grad_gain_two, (grad_gate_w, grad_up_w, grad_down))


def attn_backward(grad_middle, kept_state, attn_rows, norm_gains):
    seq_len = grad_middle.shape[0]
    model_width = grad_middle.shape[1]
    mixed_heads = kept_state["mixed_heads"]
    grad_mid_low = grad_middle.astype(jnp.bfloat16)
    grad_out_proj = contract(mixed_heads.reshape(seq_len, QD), grad_mid_low, 0, 0)
    grad_heads = contract(grad_mid_low, attn_rows[QD + 2 * KD :], 1, 1).astype(jnp.bfloat16)
    grad_heads = grad_heads.reshape(seq_len, KV_HEADS, GROUP, HEAD_DIM)
    grad_queries, grad_keys, grad_values = attend_back(
        kept_state["queries"],
        kept_state["key_rows"],
        kept_state["value_rows"],
        kept_state["allowed"],
        mixed_heads,
        kept_state["log_totals"],
        grad_heads,
    )
    cosine = kept_state["cosine"]
    sine_tab = kept_state["sine_tab"]
    grad_q_part = grad_queries.reshape(seq_len, HEADS, HEAD_DIM)
    grad_q_part = grad_q_part * cosine - rotate_half(grad_q_part) * sine_tab
    grad_k_part = grad_keys * cosine - rotate_half(grad_keys) * sine_tab
    grad_projected = jnp.concatenate(
        [
            grad_q_part.reshape(seq_len, QD),
            grad_k_part.reshape(seq_len, KD),
            grad_values.reshape(seq_len, KD),
        ],
        axis=1,
    ).astype(jnp.bfloat16)
    grad_qkv = contract(grad_projected, kept_state["input_one"], 0, 0)
    grad_input_one = contract(grad_projected, attn_rows[: QD + 2 * KD], 1, 0)
    grad_norm_one, grad_gain_one = norm_back(
        grad_input_one, kept_state["normed_one"], kept_state["inv_one"], norm_gains[:model_width]
    )
    grad_tokens = grad_middle + grad_norm_one
    grad_attn = jnp.concatenate([grad_qkv.astype(jnp.bfloat16), grad_out_proj.astype(jnp.bfloat16)], axis=0)
    return (grad_tokens, grad_attn, grad_gain_one)


MESH = pl.DeviceIdType.MESH
AXES = ("z", "y", "x")
SIZES = {"z": 4, "y": 2, "x": 2}
STRIDES = {"z": 8, "y": 4, "x": 2}
gather_orders = ("xyz", "yxz", "zxy", "zyx", "zxy", "zyx", "zxy", "zyx")


def gather_parts(rows):
    first = (rows // 2 + 15) // 16 * 16
    halves = [(0, first), (first, rows - first)]
    parts = []
    for weight in range(4):
        for half, (start, count) in enumerate(halves):
            parts.append((weight, start, count, gather_orders[2 * weight + half]))
    return parts


def place():
    me = lax.axis_index("dp")
    return {
        "me": me,
        "core": lax.rem(me, 2),
        "x": lax.rem(me // 2, 2),
        "y": lax.rem(me // 4, 2),
        "z": me // 8,
    }


def neighbours(at):
    me = at["me"]
    found = {
        "core": me + 1 - 2 * at["core"],
        "x": me + 2 - 4 * at["x"],
        "y": me + 4 - 8 * at["y"],
        "up": lax.rem(me + 8, 32),
        "down": lax.rem(me + 24, 32),
    }
    return found


def greet(near):
    barrier = pltpu.get_barrier_semaphore()
    for device in near.values():
        pl.semaphore_signal(barrier, inc=1, device_id=(device,), device_id_type=MESH)
    pl.semaphore_wait(barrier, len(near))


def arrival_order(parts, weights, reverse):
    free = {"z": 0.0, "y": 0.0, "x": 0.0, "core": 0.0}
    jobs, order, tick = [], [], 0

    def push(ready, link, size, part, phase, step):
        nonlocal tick
        tick += 1
        jobs.append((ready, tick, link, size, part, phase, step))

    def phase_size(order_of, phase):
        size = 1.0
        for axis in order_of[:phase]:
            size *= SIZES[axis]
        return size

    def begin(part, phase, ready):
        axes = parts[part][3]
        if phase < 3:
            rank = 2 - phase if reverse else phase
            link = axes[rank]
            push(ready, link, weights[part] * phase_size(axes, rank), part, phase, 0)

    for part in range(len(parts)):
        if reverse:
            push(0.0, "core", weights[part] * 16 / 6, part, -1, 0)
        else:
            begin(part, 0, 0.0)
    while jobs:
        job = min(jobs, key=lambda item: (max(item[0], free[item[2]]), item[1]))
        jobs.remove(job)
        ready, _, link, size, part, phase, step = job
        end = max(ready, free[link]) + size
        free[link] = end
        order.append((end, part, phase, step))
        if link == "z" and step < 2:
            push(end, link, size, part, phase, step + 1)
        else:
            begin(part, phase + 1, end)
    order.sort()
    return [(part, phase, step) for _, part, phase, step in order]


class Copies:
    def __init__(self, send_sems, recv_sems):
        self.send_sems, self.recv_sems = send_sems, recv_sems
        self.slots, self.pending = {}, []

    def slot(self, key):
        return self.slots.setdefault(key, len(self.slots))

    def copy(self, key, source, target, device):
        index = self.slot(key)
        return pltpu.make_async_remote_copy(
            src_ref=source,
            dst_ref=target,
            send_sem=self.send_sems.at[index],
            recv_sem=self.recv_sems.at[index],
            device_id=(device,),
            device_id_type=MESH,
        )

    def start(self, key, source, target, device, when=None):
        copy = self.copy(key, source(), target(), device)
        run, finish = copy.start, copy.wait_send

        if when is None:
            run()
            self.pending.append(finish)
        else:
            pl.when(when)(lambda: run())
            self.pending.append(lambda: pl.when(when)(lambda: finish()))

    def arrive(self, key, target, device):
        self.copy(key, target, target, device).wait_recv()

    def drain(self):
        for finish in self.pending:
            finish()


def gather_kernel(parts, events, *refs):
    count = 5
    ins, outs = refs[:count], refs[count : 2 * count]
    send_sems, recv_sems, local_sems = refs[2 * count :]
    at = place()
    near = neighbours(at)
    z = at["z"]
    copies = Copies(send_sems, recv_sems)
    locals_ = []
    for which in range(count):
        own = outs[which].at[pl.ds(z, 1), pl.ds(at["y"], 1), pl.ds(at["x"], 1), pl.ds(at["core"], 1)]
        local = pltpu.make_async_copy(ins[which], own, local_sems.at[which])
        local.start()
        locals_.append(local)
    greet(near)
    for local in locals_:
        local.wait()

    def view(part, chosen, core=None):
        weight, start, rows, _ = parts[part]
        index = []
        for axis in AXES:
            index.append(pl.ds(chosen[axis], 1) if axis in chosen else slice(None))
        index.append(pl.ds(at["core"] if core is None else core, 1))
        return outs[weight].at[tuple(index) + (pl.ds(start, rows),)]

    def fixed(part, phase):
        return {axis: at[axis] for axis in parts[part][3][phase + 1 :]}

    core_arrivals = []

    def to_partner(part, tag, chosen, when=None):
        key = (part, "core", tag)
        copies.start(
            key, lambda: view(part, chosen()), lambda: view(part, chosen()), near["core"], when
        )

        def land():
            copies.arrive(key, view(part, chosen(), 1 - at["core"]), near["core"])

        core_arrivals.append(land if when is None else (lambda: pl.when(when)(land)))

    def begin(part, phase):
        axis = parts[part][3][phase]
        chosen = dict(fixed(part, phase), **{axis: at[axis]})
        block = lambda: view(part, chosen)
        if axis == "z":
            copies.start((part, "up", 1), block, block, near["up"], z < 3)
            copies.start((part, "down", 1), block, block, near["down"], z > 0)
        else:
            copies.start((part, axis), block, block, near[axis])

    for part in range(len(parts)):
        begin(part, 0)
    for part in range(len(parts)):
        to_partner(part, "own", lambda: {axis: at[axis] for axis in AXES})

    for part, phase, step in events:
        axis = parts[part][3][phase]
        rest = fixed(part, phase)
        if axis == "z":
            hop = step + 1
            for way, sign, onward in (("up", -1, z < 3), ("down", 1, z > 0)):
                there = (z >= hop) if sign < 0 else (z + hop <= 3)
                chosen = lambda rest=rest, sign=sign, hop=hop: dict(rest, z=z + sign * hop)

                @pl.when(there)
                def _(way=way, chosen=chosen, hop=hop):
                    copies.arrive((part, way, hop), view(part, chosen()), near[way])

                if hop < 3:
                    block = lambda part=part, chosen=chosen: view(part, chosen())
                    copies.start(
                        (part, way, hop + 1), block, block, near[way], jnp.logical_and(there, onward)
                    )
                to_partner(part, (way, hop), chosen, there)
        else:
            chosen = dict(rest, **{axis: 1 - at[axis]})
            copies.arrive((part, axis), view(part, chosen), near[axis])
            to_partner(part, axis, lambda chosen=chosen: chosen)
        if (axis != "z" or step == 2) and phase < 2:
            begin(part, phase + 1)
    for land in core_arrivals:
        land()
    copies.drain()


def sized_parts(shapes):
    rows = shapes[0][-2]
    parts = gather_parts(rows) + [(4, 0, shapes[4][-2], "zxy")]
    weights = [part[2] * shapes[part[0]][-1] / (rows * shapes[0][-1]) for part in parts]
    return parts, weights


def gather_all(blocks):
    shapes = [block.shape for block in blocks]
    parts, weights = sized_parts(shapes)
    events = arrival_order(parts, weights, False)
    return pl.pallas_call(
        lambda *refs: gather_kernel(parts, events, *refs),
        out_shape=[
            jax.ShapeDtypeStruct((4, 2, 2, 2) + shape[4:], block.dtype)
            for shape, block in zip(shapes, blocks)
        ],
        in_specs=[pl.BlockSpec(memory_space=pltpu.VMEM)] * 5,
        out_specs=[pl.BlockSpec(memory_space=pl.ANY)] * 5,
        scratch_shapes=[
            pltpu.SemaphoreType.DMA((len(parts) * 18,)),
            pltpu.SemaphoreType.DMA((len(parts) * 18,)),
            pltpu.SemaphoreType.DMA((5,)),
        ],
        compiler_params=pltpu.CompilerParams(collective_id=0, has_side_effects=True),
        name="gather_all",
    )(*blocks)


def scatter_kernel(parts, events, buffers, *refs):
    count = 5
    grads, outs = refs[:count], refs[count : 2 * count]
    refs = refs[2 * count :]
    sums, landed = refs[:count], refs[count : 2 * count]
    refs = refs[2 * count :]
    bufs = dict(zip(buffers, refs[: len(buffers)]))
    send_sems, recv_sems, local_sems = refs[len(buffers) :]
    at = place()
    near = neighbours(at)
    z = at["z"]
    core = at["core"]
    copies = Copies(send_sems, recv_sems)

    def rows_of(part):
        return pl.ds(parts[part][1], parts[part][2])

    locals_ = []
    for part, (weight, *_) in enumerate(parts):
        local = pltpu.make_async_copy(
            grads[weight].at[:, :, :, pl.ds(core, 1), rows_of(part)],
            sums[weight].at[:, :, :, :, rows_of(part)],
            local_sems.at[part],
        )
        local.start()
        locals_.append(local)
    greet(near)

    def phases(part):
        return parts[part][3][::-1]

    def add_block(part, chosen, source, source_rows):
        weight, start, rows, _ = parts[part]
        target = sums[weight]
        spans = [1 if axis in chosen else SIZES[axis] for axis in AXES]
        bases = [chosen.get(axis, 0) for axis in AXES]

        def body(step, carry):
            k = step % spans[2]
            j = (step // spans[2]) % spans[1]
            i = step // (spans[2] * spans[1])
            there = (i + bases[0], j + bases[1], k + bases[2], 0, pl.ds(start, rows))
            target[there] = target[there] + source[i, j, k, 0, source_rows]
            return carry

        lax.fori_loop(0, spans[0] * spans[1] * spans[2], body, 0)

    def begin(part, phase):
        axis = phases(part)[phase]
        before = {name: at[name] for name in phases(part)[:phase]}
        weight = parts[part][0]
        target = lambda slot: bufs[(part, phase, slot)]
        if axis == "z":
            for j in range(3):
                block = lambda q, before=before: view(part, dict(before, z=q))
                copies.start((part, "up", j), lambda j=j: block(3 - j), lambda j=j: target(("up", j)), near["up"], z == 0)
                copies.start((part, "down", j), lambda j=j: block(j), lambda j=j: target(("down", j)), near["down"], z == 3)
        else:
            chosen = dict(before, **{axis: 1 - at[axis]})
            copies.start((part, axis), lambda: view(part, chosen), lambda: target(axis), near[axis])

    def view(part, chosen):
        index = []
        for axis in AXES:
            index.append(pl.ds(chosen[axis], 1) if axis in chosen else slice(None))
        return sums[parts[part][0]].at[tuple(index) + (slice(None), rows_of(part))]

    for part, (weight, *_) in enumerate(parts):
        source = lambda weight=weight, part=part: grads[weight].at[
            :, :, :, pl.ds(1 - core, 1), rows_of(part)
        ]
        target = lambda weight=weight, part=part: landed[weight].at[:, :, :, :, rows_of(part)]
        copies.start((part, "core"), source, target, near["core"])

    for part, phase, step in events:
        weight, start, rows, _ = parts[part]
        if phase < 0:
            locals_[part].wait()
            copies.arrive((part, "core"), landed[weight].at[:, :, :, :, rows_of(part)], near["core"])
            add_block(part, {}, landed[weight], rows_of(part))
            begin(part, 0)
            continue
        axis = phases(part)[phase]
        before = {name: at[name] for name in phases(part)[:phase]}
        if axis == "z":
            j = step
            ways = (
                ("up", 3 - j, (z > 0) & (j <= 3 - z), (z > 0) & (z < 3) & (j <= 2 - z)),
                ("down", j, (z < 3) & (j <= z), (z < 3) & (z > 0) & (j <= z - 1)),
            )
            for way, q, arrives, onward in ways:
                buf = bufs[(part, phase, (way, j))]

                @pl.when(arrives)
                def _(way=way, q=q, buf=buf):
                    copies.arrive((part, way, j), buf, near[way])
                    add_block(part, dict(before, z=q), buf, slice(None))

                copies.start(
                    (part, way, j),
                    lambda q=q: view(part, dict(before, z=q)),
                    lambda buf=buf: buf,
                    near[way],
                    onward,
                )
        else:
            buf = bufs[(part, phase, axis)]
            copies.arrive((part, axis), buf, near[axis])
            add_block(part, dict(before, **{axis: at[axis]}), buf, slice(None))
        if axis != "z" or step == 2:
            if phase < 2:
                begin(part, phase + 1)
            else:
                outs[weight][rows_of(part), :] = sums[weight][
                    at["z"], at["y"], at["x"], 0, rows_of(part)
                ].astype(jnp.float32)
    copies.drain()


def scatter_all(grads):
    shapes = [grad.shape for grad in grads]
    parts, weights = sized_parts(shapes)
    events = arrival_order(parts, weights, True)
    buffers, shapes_of = [], []
    for part, (weight, start, rows, order) in enumerate(parts):
        extent = dict(SIZES)
        for phase, axis in enumerate(order[::-1]):
            extent[axis] = 1
            shape = tuple(extent[name] for name in AXES) + (1, rows, shapes[weight][-1])
            names = [(way, j) for way in ("up", "down") for j in range(3)] if axis == "z" else [axis]
            for name in names:
                buffers.append((part, phase, name))
                shapes_of.append(pltpu.VMEM(shape, grads[weight].dtype))
    plane = [pltpu.VMEM((4, 2, 2, 1) + shape[4:], grad.dtype) for shape, grad in zip(shapes, grads)]
    return pl.pallas_call(
        lambda *refs: scatter_kernel(parts, events, buffers, *refs),
        out_shape=[jax.ShapeDtypeStruct(shape[4:], jnp.float32) for shape in shapes],
        in_specs=[pl.BlockSpec(memory_space=pl.ANY)] * 5,
        out_specs=[pl.BlockSpec(memory_space=pltpu.VMEM)] * 5,
        scratch_shapes=plane
        + plane
        + shapes_of
        + [
            pltpu.SemaphoreType.DMA((len(parts) * 10,)),
            pltpu.SemaphoreType.DMA((len(parts) * 10,)),
            pltpu.SemaphoreType.DMA((len(parts),)),
        ],
        compiler_params=pltpu.CompilerParams(
            collective_id=1, has_side_effects=True, vmem_limit_bytes=56 << 20
        ),
        name="scatter_all",
    )(*grads)


def gather_weights(shards, gains):
    devices = lax.axis_size("dp")
    rows, width = shards[0].shape
    if devices == 32 and rows % 16 == 0:
        gain_block = jnp.pad(gains[None, :], ((0, 15), (0, 128 - gains.shape[0])))
        blocks = [block[None, None, None, None] for block in list(shards) + [gain_block]]
        full = gather_all(blocks)
        gathered = [block.reshape(devices * rows, width) for block in full[:4]]
        return gathered, full[4].reshape(devices, 16, 128)[:, 0, : gains.shape[0]].reshape(-1)
    gathered = [lax.all_gather(shard, "dp", axis=0, tiled=True) for shard in shards]
    return gathered, lax.all_gather(gains, "dp", axis=0, tiled=True)


def scatter_grads(grads, gain_grads):
    devices = lax.axis_size("dp")
    rows = grads[0].shape[0] // devices
    width = grads[0].shape[1]
    low = [grad.astype(jnp.bfloat16) for grad in grads]
    gain_count = gain_grads.shape[0] // devices
    if devices == 32 and rows % 16 == 0:
        gain_block = jnp.pad(
            gain_grads.reshape(devices, 1, gain_count), ((0, 0), (0, 7), (0, 128 - gain_count))
        )
        blocks = [grad.reshape(4, 2, 2, 2, rows, width) for grad in low]
        shares = scatter_all(blocks + [gain_block.reshape(4, 2, 2, 2, 8, 128)])
        return shares[:4], shares[4][0, :gain_count]
    shares = [
        lax.psum_scatter(grad, "dp", scatter_dimension=0, tiled=True).astype(jnp.float32)
        for grad in low
    ]
    return shares, lax.psum_scatter(gain_grads, "dp", scatter_dimension=0, tiled=True)


def on_device(
    tokens,
    out_grad,
    segment_ids,
    positions,
    attn_weight,
    gate_weight,
    up_weight,
    down_weight,
    norm_gains,
):
    (attn_rows, gate_rows, up_rows, down_rows), gains = gather_weights(
        (attn_weight.T, gate_weight.T, up_weight.T, down_weight), norm_gains
    )
    output, kept_state = layer_forward(
        tokens, segment_ids[0], positions[0], attn_rows, gate_rows, up_rows, down_rows, gains
    )
    grad_middle, grad_gain_two, ffn_grads = ffn_backward(
        out_grad, kept_state, gate_rows, up_rows, down_rows, gains
    )
    grad_tokens, grad_attn, grad_gain_one = attn_backward(
        grad_middle, kept_state, attn_rows, gains
    )
    grad_gains = jnp.concatenate([grad_gain_one, grad_gain_two])
    shares, gain_share = scatter_grads((grad_attn,) + ffn_grads, grad_gains)
    return (
        output,
        grad_tokens,
        shares[0].T,
        shares[1].T,
        shares[2].T,
        shares[3],
        gain_share,
    )


def solution(mesh):
    in_specs = (
        P("dp", None),
        P("dp", None),
        P("dp", None),
        P("dp", None),
        P(None, "dp"),
        P(None, "dp"),
        P(None, "dp"),
        P("dp", None),
        P("dp"),
    )
    out_specs = (
        P("dp", None),
        P("dp", None),
        P(None, "dp"),
        P(None, "dp"),
        P(None, "dp"),
        P("dp", None),
        P("dp"),
    )
    return jax.shard_map(
        on_device, mesh=mesh, in_specs=in_specs, out_specs=out_specs, check_vma=False
    )
```
